32 devices in a mesh: pipe: 2 (over core), tensor: 4 (over y, x), dp: 4 (over z).
Axes of the slice: x: 2, y: 2, z: 4, core: 2. Of those that a mesh axis runs over, the one named last changes fastest.
Arguments:
- layer_input: bfloat16 [2, 512, 768], P(None, 'dp'), may hold values from -6 to 6
- enc_states: bfloat16 [2, 1024, 768], P(None, 'dp'), may hold values from -6 to 6
- out_grad: bfloat16 [2, 512, 768], P(None, 'dp'), may hold values from -6 to 6
- dec_seg: int32 [2, 512], P(None, 'dp'), may hold values from 0 to 3, as said below
- enc_seg: int32 [2, 1024], P(None, 'dp'), may hold values from 0 to 3, as said below
- buckets: int32 [128], replicated, may hold values from 0 to 31, as said below
- sa_q: bfloat16 [2, 768, 768], P('pipe', 'dp', 'tensor'), may hold values from -0.02734375 to 0.02734375
- sa_k: bfloat16 [2, 768, 768], P('pipe', 'dp', 'tensor'), may hold values from -0.21875 to 0.21875
- sa_v: bfloat16 [2, 768, 768], P('pipe', 'dp', 'tensor'), may hold values from -0.21875 to 0.21875
- sa_o: bfloat16 [2, 768, 768], P('pipe', 'tensor', 'dp'), may hold values from -0.875 to 0.875
- ca_q: bfloat16 [2, 768, 768], P('pipe', 'dp', 'tensor'), may hold values from -0.02734375 to 0.02734375
- ca_k: bfloat16 [2, 768, 768], P('pipe', 'dp', 'tensor'), may hold values from -0.21875 to 0.21875
- ca_v: bfloat16 [2, 768, 768], P('pipe', 'dp', 'tensor'), may hold values from -0.21875 to 0.21875
- ca_o: bfloat16 [2, 768, 768], P('pipe', 'tensor', 'dp'), may hold values from -0.875 to 0.875
- ff_gate: bfloat16 [2, 768, 2048], P('pipe', 'dp', 'tensor'), may hold values from -0.21875 to 0.21875
- ff_up: bfloat16 [2, 768, 2048], P('pipe', 'dp', 'tensor'), may hold values from -0.21875 to 0.21875
- ff_down: bfloat16 [2, 2048, 768], P('pipe', 'tensor', 'dp'), may hold values from -0.125 to 0.125
- norm_gains: bfloat16 [2, 3, 768], P('pipe', None, 'dp'), may hold values from 0.5 to 1.5
- rel_table: bfloat16 [2, 32, 12], P('pipe', 'dp', 'tensor'), may hold values from -4 to 4
Outputs:
- section_out: bfloat16 [2, 2, 512, 768], P('pipe', None, 'dp')
- section_in_grad: float32 [2, 2, 512, 768], P('pipe', None, 'dp')
- enc_grad: float32 [2, 2, 1024, 768], P('pipe', None, 'dp', 'tensor')
- grad_sa_q: float32 [2, 768, 768], P('pipe', 'dp', 'tensor')
- grad_sa_k: float32 [2, 768, 768], P('pipe', 'dp', 'tensor')
- grad_sa_v: float32 [2, 768, 768], P('pipe', 'dp', 'tensor')
- grad_sa_o: float32 [2, 768, 768], P('pipe', 'tensor', 'dp')
- grad_ca_q: float32 [2, 768, 768], P('pipe', 'dp', 'tensor')
- grad_ca_k: float32 [2, 768, 768], P('pipe', 'dp', 'tensor')
- grad_ca_v: float32 [2, 768, 768], P('pipe', 'dp', 'tensor')
- grad_ca_o: float32 [2, 768, 768], P('pipe', 'tensor', 'dp')
- grad_ff_gate: float32 [2, 768, 2048], P('pipe', 'dp', 'tensor')
- grad_ff_up: float32 [2, 768, 2048], P('pipe', 'dp', 'tensor')
- grad_ff_down: float32 [2, 2048, 768], P('pipe', 'tensor', 'dp')
- grad_norm_gains: float32 [2, 3, 768], P('pipe', None, 'dp')
- grad_rel_table: float32 [2, 32, 12], P('pipe', 'dp', 'tensor')
The draws below stay inside these ranges and needn't reach their ends.
Inputs may be any that keep to these rules, and one draw needn't show every extreme that they name: `dec_seg`: within each aligned block of 128 entries (one micro-batch of one group) the ids start at 0, never fall, and step up by one at exactly 3 positions. `enc_seg`: within each aligned block of 256 entries the ids start at 0, never fall, and step up by one at exactly 3 positions, so every decoder sequence has encoder tokens of its own id. `buckets`: Non-decreasing in the distance, 0 at distance 0, rising by at most one a step, and reaching 31.
All inputs are finite; a program needn't handle non-finite values.
Results may differ from the reference program's by a relative error of at most 0.033.
Values may be sent and summed in bfloat16 or wider, within the bound.
A program may use at most 128 MiB of HBM per device.

```python
from functools import partial
import jax
import jax.numpy as jnp
from jax import lax

D = 768
HEADS = 12
HEAD = 64
FF = 2048
BUCKETS = 32
MAXD = 128
INNER = 768
MB_TOK = 128
ENC_TOK = 256
SEQS = 4
MICRO = 2
SECTIONS = 2
ROWS = 512
ENC_ROWS = 1024


def segment_ids(base_key, slot_count, block_width):
    key_list = jax.random.split(base_key, slot_count)

    def cut_points(single_key):
        return jax.random.permutation(single_key, block_width - 1)[:SEQS - 1] + 1
    cut_table = jax.vmap(cut_points)(key_list)
    positions = jnp.arange(block_width, dtype=jnp.int32)
    return jnp.sum((positions[None, :, None] >= cut_table[:, None, :]).astype(jnp.int32), axis=-1).astype(jnp.int32)


def draw_dec_seg(key, part):
    return segment_ids(jax.random.fold_in(key, 11), MICRO * (ROWS // MB_TOK), MB_TOK).reshape(MICRO, ROWS)


def draw_enc_seg(key, part):
    return segment_ids(jax.random.fold_in(key, 12), MICRO * (ENC_ROWS // ENC_TOK), ENC_TOK).reshape(MICRO, ENC_ROWS)


def draw_buckets(key, part):
    cut_table = jax.random.permutation(jax.random.fold_in(key, 13), MAXD - 1)[:BUCKETS - 1] + 1
    positions = jnp.arange(MAXD, dtype=jnp.int32)
    return jnp.sum((positions[:, None] >= cut_table[None, :]).astype(jnp.int32), axis=-1).astype(jnp.int32)


def levels(key, extent, pieces, smallest, largest):
    loudness = 1.0
    for position, shards_of in pieces:
        draws = jax.random.uniform(jax.random.fold_in(jax.random.fold_in(key, 6), position), (shards_of,), jnp.float32, smallest / len(pieces), largest / len(pieces))
        loudness = loudness * jnp.repeat(jnp.exp(draws), extent[position] // shards_of).reshape((-1,) + (1,) * (len(extent) - 1 - position))
    return loudness


def bell_draw(rng, dims, deviation, most, shards=(), held_as=jnp.bfloat16):
    array = jax.random.normal(rng, dims, jnp.float32) * deviation
    if len(shards) > 0:
        array = levels(rng, dims, shards, -0.22, 0.18) * array
    return jnp.clip(array, min=-most, max=most).astype(held_as)


def setup_inputs(seed: int = 0) -> dict:
    streams_of = jax.random.split(jax.random.key(seed), 20)
    return {
        "layer_input": bell_draw(streams_of[0], (MICRO, ROWS, D), 1.0, 6.0, ((1, 4),)),
        "enc_states": bell_draw(streams_of[1], (MICRO, ENC_ROWS, D), 1.0, 6.0, ((1, 4),)),
        "out_grad": bell_draw(streams_of[2], (MICRO, ROWS, D), 1.0, 6.0, ((1, 4),)),
        "dec_seg": draw_dec_seg(jax.random.fold_in(streams_of[19], 71), 0),
        "enc_seg": draw_enc_seg(jax.random.fold_in(streams_of[19], 71), 0),
        "buckets": draw_buckets(jax.random.fold_in(streams_of[19], 71), 0),
        "sa_q": bell_draw(streams_of[6], (SECTIONS, D, INNER), (D * HEAD) ** -0.5, 0.02734375, ((0, 2), (1, 4), (2, 4))),
        "sa_k": bell_draw(streams_of[7], (SECTIONS, D, INNER), D ** -0.5, 0.21875, ((0, 2), (1, 4), (2, 4))),
        "sa_v": bell_draw(streams_of[8], (SECTIONS, D, INNER), D ** -0.5, 0.21875, ((0, 2), (1, 4), (2, 4))),
        "sa_o": bell_draw(streams_of[9], (SECTIONS, INNER, D), (INNER // 16) ** -0.5, 0.875, ((0, 2), (1, 4), (2, 4))),
        "ca_q": bell_draw(streams_of[10], (SECTIONS, D, INNER), (D * HEAD) ** -0.5, 0.02734375, ((0, 2), (1, 4), (2, 4))),
        "ca_k": bell_draw(streams_of[11], (SECTIONS, D, INNER), D ** -0.5, 0.21875, ((0, 2), (1, 4), (2, 4))),
        "ca_v": bell_draw(streams_of[12], (SECTIONS, D, INNER), D ** -0.5, 0.21875, ((0, 2), (1, 4), (2, 4))),
        "ca_o": bell_draw(streams_of[13], (SECTIONS, INNER, D), (INNER // 16) ** -0.5, 0.875, ((0, 2), (1, 4), (2, 4))),
        "ff_gate": bell_draw(streams_of[14], (SECTIONS, D, FF), D ** -0.5, 0.21875, ((0, 2), (1, 4), (2, 4))),
        "ff_up": bell_draw(streams_of[15], (SECTIONS, D, FF), D ** -0.5, 0.21875, ((0, 2), (1, 4), (2, 4))),
        "ff_down": bell_draw(streams_of[16], (SECTIONS, FF, D), FF ** -0.5, 0.125, ((0, 2), (1, 4), (2, 4))),
        "norm_gains": jnp.clip(1.0 + 0.1 * jax.random.normal(streams_of[17], (SECTIONS, 3, D), jnp.float32), 0.5, 1.5).astype(jnp.bfloat16),
        "rel_table": bell_draw(streams_of[18], (SECTIONS, BUCKETS, HEADS), 1.0, 4.0, ((0, 2), (1, 4), (2, 4))),
    }


EPS = 1e-06

def product(form, left_side, right_side):
    return jnp.einsum(form, left_side.astype(jnp.float32), right_side.astype(jnp.float32))

def rms_norm(values, gain):
    return values * lax.rsqrt(lax.optimization_barrier(jnp.mean(values * values, axis=-1, keepdims=True)) + EPS) * gain

def norm_back(values, gain, cotangent):
    _, pull_back = jax.vjp(rms_norm, values, gain)
    return pull_back(cotangent)

def gelu_tanh(values):
    return jax.nn.gelu(values, approximate=True)

def bucket_table(buckets):
    return (buckets[:, None] == jnp.arange(BUCKETS, dtype=jnp.int32)[None, :]).astype(jnp.float32)

def distance_bias(one_hot, table):
    return jnp.dot(one_hot, table.astype(jnp.float32), precision=lax.Precision.HIGHEST).T

def build_masks(dec_ids, enc_ids):
    row_count = dec_ids.shape[0]
    row_ids = jnp.arange(row_count, dtype=jnp.int32)
    allowed_self = (dec_ids[:, None] == dec_ids[None, :]) & (row_ids[None, :] <= row_ids[:, None])
    allowed_cross = dec_ids[:, None] == enc_ids[None, :]
    distance = jnp.clip(row_ids[:, None] - row_ids[None, :], 0, MAXD - 1).astype(jnp.int32)
    return (allowed_self, allowed_cross, distance)

def shard_sum(operands):
    running = None
    for left_side, right_side in operands:
        term = product('rk,kd->rd', left_side, right_side)
        running = term if running is None else running + term
    return running

def split_heads(values, head_count):
    return values.reshape(values.shape[0], head_count, values.shape[1] // head_count)

def attend(query, key_rows, value_rows, bias_block, allowed, head_count):
    query_heads = split_heads(query, head_count)
    key_heads = split_heads(key_rows, head_count)
    value_heads = split_heads(value_rows, head_count)
    scores = product('qhd,khd->hqk', query_heads, key_heads)
    if bias_block is not None:
        scores = scores + bias_block
    scores = jnp.where(allowed[None], scores, -1e+30)
    log_total = jnp.log(lax.optimization_barrier(jnp.sum(jnp.exp(scores), axis=-1, keepdims=True)))
    probs = jnp.exp(scores - log_total).astype(jnp.bfloat16)
    attended = product('hqk,khd->qhd', probs, value_heads)
    return (attended.reshape(query.shape[0], query.shape[1]).astype(jnp.bfloat16), log_total)

def attend_back(grad_attended, query, key_rows, value_rows, bias_block, allowed, log_total, attended, head_count):
    query_heads = split_heads(query, head_count)
    key_heads = split_heads(key_rows, head_count)
    value_heads = split_heads(value_rows, head_count)
    scores = product('qhd,khd->hqk', query_heads, key_heads)
    if bias_block is not None:
        scores = scores + bias_block
    scores = jnp.where(allowed[None], scores, -1e+30)
    probs = jnp.exp(scores - log_total)
    probs_low = probs.astype(jnp.bfloat16)
    grad_heads = split_heads(grad_attended, head_count)
    grad_values = product('hqk,qhd->khd', probs_low, grad_heads)
    grad_probs = product('qhd,khd->hqk', grad_heads, value_heads)
    delta = lax.optimization_barrier(jnp.sum(grad_heads.astype(jnp.float32) * split_heads(attended, head_count).astype(jnp.float32), axis=-1))
    grad_scores = probs * (grad_probs - delta.T[:, :, None])
    scores_low = grad_scores.astype(jnp.bfloat16)
    grad_query = product('hqk,khd->qhd', scores_low, key_heads)
    grad_keys = product('hqk,qhd->khd', scores_low, query_heads)
    grad_query = grad_query.reshape(query.shape).astype(jnp.bfloat16)
    grad_keys = grad_keys.reshape(key_rows.shape).astype(jnp.bfloat16)
    grad_values = grad_values.reshape(value_rows.shape).astype(jnp.bfloat16)
    return (grad_query, grad_keys, grad_values, grad_scores)

def layer_forward(hidden_in, enc_block, allowed_self, allowed_cross, bias_block, weights, reduce_sum):
    w_query, w_key, w_value, c_query, c_key, c_value, w_gate, w_up, w_out, c_out, w_down, gains = weights
    head_count = w_query.shape[1] // HEAD
    resid_zero = hidden_in.astype(jnp.float32)
    normed_one = rms_norm(resid_zero, gains[0]).astype(jnp.bfloat16)
    self_query = product('rd,di->ri', normed_one, w_query).astype(jnp.bfloat16)
    self_keys = product('rd,di->ri', normed_one, w_key).astype(jnp.bfloat16)
    self_values = product('rd,di->ri', normed_one, w_value).astype(jnp.bfloat16)
    self_out, self_lse = attend(self_query, self_keys, self_values, bias_block, allowed_self, head_count)
    resid_one = resid_zero + reduce_sum(((self_out, w_out),))
    normed_two = rms_norm(resid_one, gains[1]).astype(jnp.bfloat16)
    cross_query = product('rd,di->ri', normed_two, c_query).astype(jnp.bfloat16)
    cross_keys = product('ed,di->ei', enc_block, c_key).astype(jnp.bfloat16)
    cross_values = product('ed,di->ei', enc_block, c_value).astype(jnp.bfloat16)
    cross_out, cross_lse = attend(cross_query, cross_keys, cross_values, None, allowed_cross, head_count)
    resid_two = resid_one + reduce_sum(((cross_out, c_out),))
    normed_three = rms_norm(resid_two, gains[2]).astype(jnp.bfloat16)
    gate_pre = product('rd,df->rf', normed_three, w_gate)
    up_pre = product('rd,df->rf', normed_three, w_up)
    hidden = (gelu_tanh(gate_pre) * up_pre).astype(jnp.bfloat16)
    result = resid_two + reduce_sum(((hidden, w_down),))
    saved_state = (normed_one, self_query, self_keys, self_values, self_lse, self_out, resid_one, normed_two, cross_query, cross_keys, cross_values, cross_lse, cross_out, resid_two, normed_three, gate_pre, up_pre, hidden)
    return (result, saved_state)

def layer_backward(grad_out, hidden_in, enc_block, saved_state, allowed_self, allowed_cross, bias_block, distance, weights, reduce_sum):
    w_query, w_key, w_value, c_query, c_key, c_value, w_gate, w_up, w_out, c_out, w_down, gains = weights
    normed_one, self_query, self_keys, self_values, self_lse, self_out, resid_one, normed_two, cross_query, cross_keys, cross_values, cross_lse, cross_out, resid_two, normed_three, gate_pre, up_pre, hidden = saved_state
    head_count = w_query.shape[1] // HEAD
    resid_zero = hidden_in.astype(jnp.float32)
    grad_three_low = grad_out.astype(jnp.bfloat16)
    grad_down = product('rf,rd->fd', hidden, grad_three_low)
    grad_hidden = product('rd,fd->rf', grad_three_low, w_down)
    gelu_value, gelu_pull = jax.vjp(gelu_tanh, gate_pre)
    grad_gate_pre = gelu_pull(grad_hidden * up_pre)[0].astype(jnp.bfloat16)
    grad_up_pre = (grad_hidden * gelu_value).astype(jnp.bfloat16)
    grad_gate = product('rd,rf->df', normed_three, grad_gate_pre)
    grad_up = product('rd,rf->df', normed_three, grad_up_pre)
    grad_normed = reduce_sum(((grad_gate_pre, w_gate.T), (grad_up_pre, w_up.T)))
    back_three, gain_three = norm_back(resid_two, gains[2], grad_normed)
    grad_two = grad_out + back_three
    grad_two_low = grad_two.astype(jnp.bfloat16)
    grad_c_out = product('ri,rd->id', cross_out, grad_two_low)
    grad_cross = product('rd,id->ri', grad_two_low, c_out).astype(jnp.bfloat16)
    grad_cross_query, grad_cross_keys, grad_cross_values, _ = attend_back(grad_cross, cross_query, cross_keys, cross_values, None, allowed_cross, cross_lse, cross_out, head_count)
    grad_c_query = product('rd,ri->di', normed_two, grad_cross_query)
    grad_c_key = product('ed,ei->di', enc_block, grad_cross_keys)
    grad_c_value = product('ed,ei->di', enc_block, grad_cross_values)
    grad_enc = product('ei,di->ed', grad_cross_keys, c_key) + product('ei,di->ed', grad_cross_values, c_value)
    grad_normed = reduce_sum(((grad_cross_query, c_query.T),))
    back_two, gain_two = norm_back(resid_one, gains[1], grad_normed)
    grad_one = grad_two + back_two
    grad_one_low = grad_one.astype(jnp.bfloat16)
    grad_w_out = product('ri,rd->id', self_out, grad_one_low)
    grad_self = product('rd,id->ri', grad_one_low, w_out).astype(jnp.bfloat16)
    grad_query, grad_keys, grad_values, grad_scores = attend_back(grad_self, self_query, self_keys, self_values, bias_block, allowed_self, self_lse, self_out, head_count)
    grad_distance = jax.ops.segment_sum(grad_scores.reshape(head_count, -1).T, distance.reshape(-1), num_segments=MAXD)
    grad_w_query = product('rd,ri->di', normed_one, grad_query)
    grad_w_key = product('rd,ri->di', normed_one, grad_keys)
    grad_w_value = product('rd,ri->di', normed_one, grad_values)
    grad_normed = reduce_sum(((grad_query, w_query.T), (grad_keys, w_key.T), (grad_values, w_value.T)))
    back_one, gain_one = norm_back(resid_zero, gains[0], grad_normed)
    grad_input = grad_one + back_one
    grads = (grad_w_query, grad_w_key, grad_w_value, grad_c_query, grad_c_key, grad_c_value, grad_gate, grad_up, grad_w_out, grad_c_out, grad_down, jnp.stack([gain_one, gain_two, gain_three]), grad_distance)
    return (grad_input, grad_enc, grads)

def zero_grads(inner_width, hidden_width, head_count):
    return (jnp.zeros((D, inner_width), jnp.float32),) * 6 + (jnp.zeros((D, hidden_width), jnp.float32),) * 2 + (jnp.zeros((inner_width, D), jnp.float32),) * 2 + (jnp.zeros((hidden_width, D), jnp.float32), jnp.zeros((3, D), jnp.float32), jnp.zeros((MAXD, head_count), jnp.float32))

def forward_slot(weights, by_dist, slot_item):
    hidden_in, enc_block, dec_ids, enc_ids = slot_item
    allowed_self, allowed_cross, distance = build_masks(dec_ids, enc_ids)
    bias_block = jnp.take(by_dist, distance, axis=1)
    result, _ = layer_forward(hidden_in, enc_block, allowed_self, allowed_cross, bias_block, weights, shard_sum)
    return result.astype(jnp.bfloat16)

def backward_slot(weights, by_dist, carried, slot_item):
    hidden_in, enc_block, dec_ids, enc_ids, upstream = slot_item
    allowed_self, allowed_cross, distance = build_masks(dec_ids, enc_ids)
    bias_block = jnp.take(by_dist, distance, axis=1)
    _, saved_state = layer_forward(hidden_in, enc_block, allowed_self, allowed_cross, bias_block, weights, shard_sum)
    grad_input, grad_enc, grads = layer_backward(upstream, hidden_in, enc_block, saved_state, allowed_self, allowed_cross, bias_block, distance, weights, shard_sum)
    return (jax.tree.map(lambda a, b: a + b, carried, grads), (grad_input, grad_enc))

def reference(layer_input, enc_states, out_grad, dec_seg, enc_seg, buckets, sa_q, sa_k, sa_v, sa_o, ca_q, ca_k, ca_v, ca_o, ff_gate, ff_up, ff_down, norm_gains, rel_table):
    slot_count = ROWS // MB_TOK
    inputs_now = layer_input.reshape(MICRO, slot_count, MB_TOK, D)
    encoder = enc_states.reshape(MICRO, slot_count, ENC_TOK, D)
    dec_ids = dec_seg.reshape(MICRO, slot_count, MB_TOK)
    enc_ids = enc_seg.reshape(MICRO, slot_count, ENC_TOK)
    one_hot = bucket_table(buckets)
    section_weights = []
    section_bias = []
    for section_id in range(SECTIONS):
        section_weights.append((sa_q[section_id], sa_k[section_id], sa_v[section_id], ca_q[section_id], ca_k[section_id], ca_v[section_id], ff_gate[section_id], ff_up[section_id], sa_o[section_id], ca_o[section_id], ff_down[section_id], norm_gains[section_id].astype(jnp.float32)))
        section_bias.append(distance_bias(one_hot, rel_table[section_id]))
    section_inputs = []
    section_outputs = []
    for section_id in range(SECTIONS):
        runner = partial(forward_slot, section_weights[section_id], section_bias[section_id])
        outputs = jnp.stack([lax.map(runner, (inputs_now[micro_id], encoder[micro_id], dec_ids[micro_id], enc_ids[micro_id])) for micro_id in range(MICRO)])
        section_inputs.append(inputs_now)
        section_outputs.append(outputs)
        inputs_now = outputs
    cotangent = out_grad.reshape(MICRO, slot_count, MB_TOK, D).astype(jnp.float32)
    in_grads = [None] * SECTIONS
    enc_grads = [None] * SECTIONS
    all_grads = [None] * SECTIONS
    for section_id in reversed(range(SECTIONS)):
        runner = partial(backward_slot, section_weights[section_id], section_bias[section_id])
        carried = zero_grads(INNER, FF, HEADS)
        micro_inputs = []
        micro_enc = []
        for micro_id in range(MICRO):
            carried, (grad_input, grad_enc) = lax.scan(runner, carried, (section_inputs[section_id][micro_id], encoder[micro_id], dec_ids[micro_id], enc_ids[micro_id], cotangent[micro_id]))
            micro_inputs.append(grad_input)
            micro_enc.append(grad_enc)
        grad_stack = jnp.stack(micro_inputs)
        in_grads[section_id] = grad_stack.reshape(MICRO, ROWS, D)
        enc_grads[section_id] = jnp.stack(micro_enc).reshape(MICRO, ENC_ROWS, D)
        table_grad = jnp.dot(one_hot.T, carried[12], precision=lax.Precision.HIGHEST)
        all_grads[section_id] = carried[:12] + (table_grad,)
        cotangent = lax.optimization_barrier(grad_stack.astype(jnp.bfloat16)).astype(jnp.float32)
    stacked = [jnp.stack([all_grads[section_id][index] for section_id in range(SECTIONS)]) for index in range(13)]
    section_out = jnp.stack([outputs.reshape(MICRO, ROWS, D) for outputs in section_outputs])
    return (section_out, jnp.stack(in_grads), jnp.stack(enc_grads), stacked[0], stacked[1], stacked[2], stacked[8], stacked[3], stacked[4], stacked[5], stacked[9], stacked[6], stacked[7], stacked[10], stacked[11], stacked[12])
```

```python
import functools

import jax
import jax.numpy as jnp
from jax import lax
from jax.experimental import pallas as pl
from jax.experimental.pallas import tpu as pltpu
from jax.sharding import PartitionSpec as P

D = 768
HEAD = 64
BUCKETS = 32
MAXD = 128
EPS = 1e-06
TAIL = 128

F32 = jnp.float32
BF16 = jnp.bfloat16
MESH = pl.DeviceIdType.MESH


def dot_nn(a, b):
    return lax.dot_general(a, b, (((1,), (0,)), ((), ())), preferred_element_type=F32)


def dot_nt(a, b):
    return lax.dot_general(a, b, (((1,), (1,)), ((), ())), preferred_element_type=F32)


def dot_tn(a, b):
    return lax.dot_general(a, b, (((0,), (0,)), ((), ())), preferred_element_type=F32)


def norm_scale(values):
    return lax.rsqrt(jnp.mean(values * values, axis=-1, keepdims=True) + EPS)


def norm_back(values, gain, cotangent):
    scale = norm_scale(values)
    scaled = cotangent * gain
    inner = jnp.mean(scaled * values, axis=-1, keepdims=True)
    back = scale * scaled - values * (scale * scale * scale * inner)
    gain_grad = jnp.sum(cotangent * values * scale, axis=0, keepdims=True)
    return back, gain_grad


def gelu_parts(u):
    root = 0.7978845608028654
    cube = 0.044715
    t = jnp.tanh(root * (u + cube * u * u * u))
    value = 0.5 * u * (1.0 + t)
    slope = 0.5 * (1.0 + t) + 0.5 * u * (1.0 - t * t) * (root * (1.0 + 3.0 * cube * u * u))
    return value, slope


def head_masks(heads):
    lane = lax.broadcasted_iota(jnp.int32, (1, heads * HEAD), 1)
    return [
        ((lane >= h * HEAD) & (lane < (h + 1) * HEAD)).astype(F32).astype(BF16)
        for h in range(heads)
    ]


def spread_heads(values, masks):
    return jnp.concatenate([values * m for m in masks], axis=0)


def join_heads(values, masks):
    rows = values.shape[0] // len(masks)
    total = None
    for h, m in enumerate(masks):
        term = values[h * rows : (h + 1) * rows] * m.astype(F32)
        total = term if total is None else total + term
    return total


def main_kernel(
    dims,
    h_ref,
    enc_ref,
    up_ref,
    w_ref,
    gain_ref,
    bias_ref,
    cmask_ref,
    bmap_ref,
    out_ref,
    ingrad_ref,
    encgrad_ref,
    grad_ref,
    gaingrad_ref,
    table_ref,
    x_in,
    g_in,
    r_one,
    r_two,
    n_one,
    n_two,
    n_three,
    qkv_s,
    so_s,
    p_s,
    cq_s,
    ckv_s,
    co_s,
    pc_s,
    gu_s,
    hid_s,
    send_one,
    recv_one,
    send_two,
    recv_two,
    enc_send,
    enc_own,
    enc_recv,
    sem_send,
    sem_recv,
    sem_enc_send,
    sem_enc_recv,
):
    layers, rows, inner, ff, heads = dims
    half = rows // 2
    t = lax.axis_index("tensor")
    near = t + 1 - 2 * (t % 2)
    far = t + 2 - 4 * ((t // 2) % 2)
    both = far + 1 - 2 * (far % 2)
    peers = (near, far, both)
    masks = head_masks(heads)
    c_q = 3 * ff
    c_so = c_q + 3 * inner
    c_cq = c_q + 4 * inner
    c_ck = c_q + 5 * inner
    c_cv = c_q + 6 * inner
    c_co = c_q + 7 * inner
    c_end = c_q + 8 * inner

    barrier = pltpu.get_barrier_semaphore()
    for peer in peers:
        pl.semaphore_signal(barrier, inc=1, device_id={"tensor": peer}, device_id_type=MESH)
    pl.semaphore_wait(barrier, 3)

    def copy_to(src, dst, sem_a, sem_b, peer):
        return pltpu.make_async_remote_copy(
            src_ref=src,
            dst_ref=dst,
            send_sem=sem_a,
            recv_sem=sem_b,
            device_id={"tensor": peer},
            device_id_type=MESH,
        )

    def all_sum(slot, make_half, cover):
        firsts = []
        for part in range(2):
            value = make_half(part).astype(BF16)
            send_one[slot, part] = value
            copy = copy_to(
                send_one.at[slot, part],
                recv_one.at[slot, part],
                sem_send.at[slot, part],
                sem_recv.at[slot, part],
                near if part == 0 else far,
            )
            copy.start()
            firsts.append(copy)
        if cover is not None:
            cover()
        seconds = []
        for part in range(2):
            firsts[part].wait()
            value = send_one[slot, part].astype(F32) + recv_one[slot, part].astype(F32)
            send_two[slot, part] = value.astype(BF16)
            copy = copy_to(
                send_two.at[slot, part],
                recv_two.at[slot, part],
                sem_send.at[slot, part + 2],
                sem_recv.at[slot, part + 2],
                far if part == 0 else near,
            )
            copy.start()
            seconds.append(copy)
        pieces = []
        for part in range(2):
            seconds[part].wait()
            pieces.append(send_two[slot, part].astype(F32) + recv_two[slot, part].astype(F32))
        return jnp.concatenate(pieces, axis=0)

    x_in[0] = h_ref[...]

    def forward(l, carry):
        x0 = x_in[l].astype(F32)
        n1 = (x0 * norm_scale(x0) * gain_ref[l, 0:1]).astype(BF16)
        n_one[l] = n1
        qkv = dot_nn(n1, w_ref[l, :, c_q:c_so]).astype(BF16)
        qkv_s[l] = qkv
        q = qkv[:, :inner]
        k = qkv[:, inner : 2 * inner]
        v = qkv[:, 2 * inner :]
        e = jnp.exp(dot_nt(spread_heads(q, masks), k) + bias_ref[l])
        p = e * (1.0 / jnp.sum(e, axis=-1, keepdims=True))
        p_s[l] = p
        so_s[l] = join_heads(dot_nn(p.astype(BF16), v), masks).astype(BF16)

        def make_one(part):
            return dot_nt(
                so_s[l, part * half : (part + 1) * half], w_ref[l, :, c_so:c_cq]
            )

        def cover_one():
            ckv_s[l] = dot_nn(enc_ref[...], w_ref[l, :, c_ck:c_co]).astype(BF16)

        x1 = x0 + all_sum(3 * l, make_one, cover_one)
        r_one[l] = x1
        n2 = (x1 * norm_scale(x1) * gain_ref[l, 1:2]).astype(BF16)
        n_two[l] = n2
        cq = dot_nn(n2, w_ref[l, :, c_cq:c_ck]).astype(BF16)
        cq_s[l] = cq
        ckv = ckv_s[l]
        ck = ckv[:, :inner]
        cv = ckv[:, inner:]
        cmask = cmask_ref[...]
        e = jnp.exp(
            dot_nt(spread_heads(cq, masks), ck) + jnp.concatenate([cmask] * heads, axis=0)
        )
        p = e * (1.0 / jnp.sum(e, axis=-1, keepdims=True))
        pc_s[l] = p
        co_s[l] = join_heads(dot_nn(p.astype(BF16), cv), masks).astype(BF16)

        def make_two(part):
            return dot_nt(
                co_s[l, part * half : (part + 1) * half], w_ref[l, :, c_co:c_end]
            )

        x2 = x1 + all_sum(3 * l + 1, make_two, None)
        r_two[l] = x2
        n3 = (x2 * norm_scale(x2) * gain_ref[l, 2:3]).astype(BF16)
        n_three[l] = n3
        gu = dot_nn(n3, w_ref[l, :, 0 : 2 * ff])
        gu_s[l] = gu
        value, _ = gelu_parts(gu[:, :ff])
        hid_s[l] = (value * gu[:, ff:]).astype(BF16)

        def make_three(part):
            return dot_nt(
                hid_s[l, part * half : (part + 1) * half], w_ref[l, :, 2 * ff : 3 * ff]
            )

        result = (x2 + all_sum(3 * l + 2, make_three, None)).astype(BF16)
        out_ref[l] = result
        x_in[l + 1] = result
        return carry

    lax.fori_loop(0, layers, forward, 0)
    g_in[...] = up_ref[...]

    def attend_back(grad, query, keys, values, attended, p):
        gs = spread_heads(grad, masks)
        qs = spread_heads(query, masks)
        delta = jnp.sum(
            gs.astype(F32) * jnp.concatenate([attended.astype(F32)] * heads, axis=0),
            axis=-1,
            keepdims=True,
        )
        ds = p * (dot_nt(gs, values) - delta)
        dsb = ds.astype(BF16)
        grad_query = join_heads(dot_nn(dsb, keys), masks).astype(BF16)
        return grad_query, ds, dsb, gs, qs

    def backward(step, carry):
        l = layers - 1 - step
        base = 3 * layers + 3 * step
        g3 = g_in[...]
        g = g3.astype(F32)
        gu = gu_s[l]
        value, slope = gelu_parts(gu[:, :ff])
        dh = dot_nn(g3, w_ref[l, :, 2 * ff : 3 * ff])
        dgu = jnp.concatenate(
            [(dh * gu[:, ff:] * slope).astype(BF16), (dh * value).astype(BF16)], axis=1
        )

        def make_three(part):
            return dot_nt(dgu[part * half : (part + 1) * half], w_ref[l, :, 0 : 2 * ff])

        def cover_three():
            grad_ref[l, :, 0 : 2 * ff] = dot_tn(n_three[l], dgu).astype(BF16)
            grad_ref[l, :, 2 * ff : 3 * ff] = dot_tn(g3, hid_s[l]).astype(BF16)

        dn = all_sum(base, make_three, cover_three)
        back, gain_three = norm_back(r_two[l], gain_ref[l, 2:3], dn)
        gaingrad_ref[l, 2:3] = gain_three
        g2 = g + back
        g2b = g2.astype(BF16)
        dc = dot_nn(g2b, w_ref[l, :, c_co:c_end]).astype(BF16)
        ckv = ckv_s[l]
        co = co_s[l]
        pc = pc_s[l]
        dcq, _, dsb, gs, qs = attend_back(dc, cq_s[l], ckv[:, :inner], ckv[:, inner:], co, pc)

        def make_two(part):
            return dot_nt(dcq[part * half : (part + 1) * half], w_ref[l, :, c_cq:c_ck])

        def cover_two():
            dck = dot_tn(dsb, qs).astype(BF16)
            dcv = dot_tn(pc.astype(BF16), gs).astype(BF16)
            dckv = jnp.concatenate([dck, dcv], axis=1)
            tsize = D // inner
            for k in range(tsize):
                owner = t if k == 0 else peers[k - 1]
                start = pl.multiple_of(owner * inner, HEAD)
                chunk = dot_nt(dckv, w_ref[l, pl.ds(start, inner), c_ck:c_co])
                if k == 0:
                    enc_own[l] = chunk
                else:
                    enc_send[l, k - 1] = chunk.astype(BF16)
                    copy_to(
                        enc_send.at[l, k - 1],
                        enc_recv.at[l, k - 1],
                        sem_enc_send.at[l, k - 1],
                        sem_enc_recv.at[l, k - 1],
                        peers[k - 1],
                    ).start()
            enc = enc_ref[...]
            block = jnp.concatenate([dot_tn(n_two[l], dcq), dot_tn(enc, dckv)], axis=1)
            grad_ref[l, :, c_cq:c_co] = block.astype(BF16)
            grad_ref[l, :, c_co:c_end] = dot_tn(g2b, co).astype(BF16)

        dn = all_sum(base + 1, make_two, cover_two)
        back, gain_two = norm_back(r_one[l], gain_ref[l, 1:2], dn)
        gaingrad_ref[l, 1:2] = gain_two
        g1 = g2 + back
        g1b = g1.astype(BF16)
        dself = dot_nn(g1b, w_ref[l, :, c_so:c_cq]).astype(BF16)
        qkv = qkv_s[l]
        so = so_s[l]
        ps = p_s[l]
        dq, ds, dsb, gs, qs = attend_back(
            dself, qkv[:, :inner], qkv[:, inner : 2 * inner], qkv[:, 2 * inner :], so, ps
        )
        dk = dot_tn(dsb, qs).astype(BF16)
        dv = dot_tn(ps.astype(BF16), gs).astype(BF16)
        dqkv = jnp.concatenate([dq, dk, dv], axis=1)

        def make_one(part):
            return dot_nt(dqkv[part * half : (part + 1) * half], w_ref[l, :, c_q:c_so])

        def cover_one():
            grad_ref[l, :, c_q:c_cq] = jnp.concatenate(
                [dot_tn(n_one[l], dqkv), dot_tn(g1b, so)], axis=1
            ).astype(BF16)
            bmap = bmap_ref[...]
            for h in range(heads):
                ds_h = ds[h * rows : (h + 1) * rows]
                for b in range(BUCKETS):
                    table_ref[l, h, b : b + 1] = jnp.sum(
                        jnp.where(bmap == b, ds_h, 0.0), axis=0, keepdims=True
                    )

        dn = all_sum(base + 2, make_one, cover_one)
        back, gain_one = norm_back(x_in[l].astype(F32), gain_ref[l, 0:1], dn)
        gaingrad_ref[l, 0:1] = gain_one
        gin = g1 + back
        ingrad_ref[l] = gin
        g_in[...] = gin.astype(BF16)
        return carry

    lax.fori_loop(0, layers, backward, 0)
    for l in range(layers):
        total = enc_own[l]
        for k in range(3):
            copy_to(
                enc_send.at[l, k],
                enc_recv.at[l, k],
                sem_enc_send.at[l, k],
                sem_enc_recv.at[l, k],
                peers[k],
            ).wait()
            total = total + enc_recv[l, k].astype(F32)
        encgrad_ref[l] = total


def run_main(h, enc, up, w, gains, bias, cmask, bmap, inner, ff):
    layers, width = w.shape[0], w.shape[2]
    rows, enc_rows = h.shape[0], enc.shape[0]
    heads = inner // HEAD
    half = rows // 2
    slots = 6 * layers
    vm = pltpu.VMEM
    dims = (layers, rows, inner, ff, heads)
    return pl.pallas_call(
        functools.partial(main_kernel, dims),
        out_shape=(
            jax.ShapeDtypeStruct((layers, rows, D), BF16),
            jax.ShapeDtypeStruct((layers, rows, D), F32),
            jax.ShapeDtypeStruct((layers, enc_rows, inner), F32),
            jax.ShapeDtypeStruct((layers, D, width), BF16),
            jax.ShapeDtypeStruct((layers, 3, D), F32),
            jax.ShapeDtypeStruct((layers, heads, BUCKETS, rows), F32),
        ),
        in_specs=[pl.BlockSpec(memory_space=pltpu.VMEM)] * 8,
        out_specs=(pl.BlockSpec(memory_space=pltpu.VMEM),) * 6,
        scratch_shapes=[
            vm((layers + 1, rows, D), BF16),
            vm((rows, D), BF16),
            vm((layers, rows, D), F32),
            vm((layers, rows, D), F32),
            vm((layers, rows, D), BF16),
            vm((layers, rows, D), BF16),
            vm((layers, rows, D), BF16),
            vm((layers, rows, 3 * inner), BF16),
            vm((layers, rows, inner), BF16),
            vm((layers, heads * rows, rows), F32),
            vm((layers, rows, inner), BF16),
            vm((layers, enc_rows, 2 * inner), BF16),
            vm((layers, rows, inner), BF16),
            vm((layers, heads * rows, enc_rows), F32),
            vm((layers, rows, 2 * ff), F32),
            vm((layers, rows, ff), BF16),
            vm((slots, 2, half, D), BF16),
            vm((slots, 2, half, D), BF16),
            vm((slots, 2, half, D), BF16),
            vm((slots, 2, half, D), BF16),
            vm((layers, 3, enc_rows, inner), BF16),
            vm((layers, enc_rows, inner), F32),
            vm((layers, 3, enc_rows, inner), BF16),
            pltpu.SemaphoreType.DMA((slots, 4)),
            pltpu.SemaphoreType.DMA((slots, 4)),
            pltpu.SemaphoreType.DMA((layers, 3)),
            pltpu.SemaphoreType.DMA((layers, 3)),
        ],
        compiler_params=pltpu.CompilerParams(
            collective_id=0, has_side_effects=True, vmem_limit_bytes=60 * 1024 * 1024
        ),
    )(h, enc, up, w, gains, bias, cmask, bmap)


def body(
    layer_input,
    enc_states,
    out_grad,
    dec_seg,
    enc_seg,
    buckets,
    sa_q,
    sa_k,
    sa_v,
    sa_o,
    ca_q,
    ca_k,
    ca_v,
    ca_o,
    ff_gate,
    ff_up,
    ff_down,
    norm_gains,
    rel_table,
):
    layers = lax.axis_size("pipe")
    dp = lax.axis_size("dp")
    mine = lax.axis_index("pipe")
    rows = layer_input.shape[1]
    inner, ff = sa_q.shape[2], ff_gate.shape[2]
    heads = inner // HEAD
    chunk, table_rows = sa_q.shape[1], rel_table.shape[1]

    def swap(value):
        return lax.ppermute(value, "pipe", [(0, 1), (1, 0)])

    tail = jnp.zeros((chunk, TAIL), BF16)
    tail = lax.dynamic_update_slice(tail, norm_gains[0].T, (0, 0))
    tail = lax.dynamic_update_slice(tail, rel_table[0], (0, 3))
    packed = jnp.concatenate(
        [
            ff_gate[0],
            ff_up[0],
            ff_down[0].T,
            sa_q[0],
            sa_k[0],
            sa_v[0],
            sa_o[0].T,
            ca_q[0],
            ca_k[0],
            ca_v[0],
            ca_o[0].T,
            tail,
        ],
        axis=1,
    )
    width = packed.shape[1]
    w = lax.all_gather(packed, ("pipe", "dp"), axis=0, tiled=True).reshape(layers, D, width)
    tails = w[:, :, width - TAIL :].astype(F32)
    gains = tails[:, :, 0:3].transpose(0, 2, 1)
    table = tails.reshape(layers, dp, chunk, TAIL)[:, :, :table_rows, 3 : 3 + heads]
    table = table.reshape(layers, BUCKETS, heads)

    dec_ids = lax.dynamic_index_in_dim(dec_seg, mine, 0, keepdims=False)
    enc_ids = lax.dynamic_index_in_dim(enc_seg, mine, 0, keepdims=False)
    row_ids = jnp.arange(rows, dtype=jnp.int32)
    allowed_self = (dec_ids[:, None] == dec_ids[None, :]) & (row_ids[None, :] <= row_ids[:, None])
    cmask = jnp.where(dec_ids[:, None] == enc_ids[None, :], 0.0, -1e30).astype(F32)
    distance = jnp.clip(row_ids[:, None] - row_ids[None, :], 0, MAXD - 1)
    bucket_ids = jnp.arange(BUCKETS, dtype=jnp.int32)
    starts = jnp.sum((buckets[None, :] < bucket_ids[1:, None]).astype(jnp.int32), axis=1)
    bmap = jnp.sum((distance[None] >= starts[:, None, None]).astype(jnp.int32), axis=0)
    bias = jnp.sum(
        jnp.where(
            bmap[None, None, None] == bucket_ids[:, None, None, None, None],
            table.transpose(1, 0, 2)[:, :, :, None, None],
            0.0,
        ),
        axis=0,
    )
    bias = jnp.where(allowed_self[None, None], bias, -1e30).reshape(layers, heads * rows, rows)

    h = lax.dynamic_index_in_dim(layer_input, mine, 0, keepdims=False)
    enc = lax.dynamic_index_in_dim(enc_states, mine, 0, keepdims=False)
    up = lax.dynamic_index_in_dim(out_grad, mine, 0, keepdims=False)
    outs, ingrads, encgrads, grads, gain_grads, table_grads = run_main(
        h, enc, up, w, gains, bias, cmask, bmap, inner, ff
    )

    def by_micro(values, sent_type):
        own = lax.dynamic_index_in_dim(values, mine, 0, keepdims=False)
        away = lax.dynamic_index_in_dim(values, 1 - mine, 0, keepdims=False)
        got = swap(away.astype(sent_type)).astype(values.dtype)
        first = jnp.where(mine == 0, own, got)
        second = jnp.where(mine == 0, got, own)
        return jnp.stack([first, second])[None]

    table_grads = jnp.sum(table_grads, axis=-1).transpose(0, 2, 1)
    table_grads = table_grads.reshape(layers, dp, table_rows, heads)
    table_grads = jnp.pad(table_grads, ((0, 0), (0, 0), (0, chunk - table_rows), (0, 0)))
    tail_grads = jnp.concatenate(
        [gain_grads.transpose(0, 2, 1), table_grads.reshape(layers, D, heads)], axis=2
    )
    tail_grads = jnp.pad(tail_grads, ((0, 0), (0, 0), (0, TAIL - 3 - heads))).astype(BF16)
    grads = lax.dynamic_update_slice(grads, tail_grads, (0, 0, width - TAIL))
    summed = lax.psum_scatter(
        grads.reshape(layers * D, width), ("pipe", "dp"), scatter_dimension=0, tiled=True
    ).astype(F32)
    base = 3 * ff

    def cut(index):
        return summed[:, base + index * inner : base + (index + 1) * inner]

    return (
        by_micro(outs, BF16),
        by_micro(ingrads, BF16),
        by_micro(encgrads, BF16),
        cut(0)[None],
        cut(1)[None],
        cut(2)[None],
        cut(3).T[None],
        cut(4)[None],
        cut(5)[None],
        cut(6)[None],
        cut(7).T[None],
        summed[None, :, 0:ff],
        summed[None, :, ff : 2 * ff],
        summed[:, 2 * ff : 3 * ff].T[None],
        summed[:, width - TAIL : width - TAIL + 3].T[None],
        summed[:table_rows, width - TAIL + 3 : width - TAIL + 3 + heads][None],
    )


def solution(mesh):
    inner_spec = P("pipe", "dp", "tensor")
    outer_spec = P("pipe", "tensor", "dp")
    placed = (
        P(None, "dp", None),
        P(None, "dp", None),
        P(None, "dp", None),
        P(None, "dp"),
        P(None, "dp"),
        P(),
        inner_spec,
        inner_spec,
        inner_spec,
        outer_spec,
        inner_spec,
        inner_spec,
        inner_spec,
        outer_spec,
        inner_spec,
        inner_spec,
        outer_spec,
        P("pipe", None, "dp"),
        inner_spec,
    )
    return jax.shard_map(
        body,
        mesh=mesh,
        in_specs=placed,
        out_specs=(
            P("pipe", None, "dp", None),
            P("pipe", None, "dp", None),
            P("pipe", None, "dp", "tensor"),
            inner_spec,
            inner_spec,
            inner_spec,
            outer_spec,
            inner_spec,
            inner_spec,
            inner_spec,
            outer_spec,
            inner_spec,
            inner_spec,
            outer_spec,
            P("pipe", None, "dp"),
            inner_spec,
        ),
        check_vma=False,
    )
```

```python
import functools

import jax
import jax.numpy as jnp
from jax import lax
from jax.experimental import pallas as pl
from jax.experimental.pallas import tpu as pltpu
from jax.sharding import PartitionSpec as P

D = 768
HEAD = 64
BUCKETS = 32
MAXD = 128
EPS = 1e-06
TAIL = 128

F32 = jnp.float32
BF16 = jnp.bfloat16
MESH = pl.DeviceIdType.MESH


def dot_nn(a, b):
    return lax.dot_general(a, b, (((1,), (0,)), ((), ())), preferred_element_type=F32)


def dot_nt(a, b):
    return lax.dot_general(a, b, (((1,), (1,)), ((), ())), preferred_element_type=F32)


def dot_tn(a, b):
    return lax.dot_general(a, b, (((0,), (0,)), ((), ())), preferred_element_type=F32)


def norm_scale(values):
    return lax.rsqrt(jnp.mean(values * values, axis=-1, keepdims=True) + EPS)


def norm_back(values, gain, cotangent):
    scale = norm_scale(values)
    scaled = cotangent * gain
    inner = jnp.mean(scaled * values, axis=-1, keepdims=True)
    back = scale * scaled - values * (scale * scale * scale * inner)
    gain_grad = jnp.sum(cotangent * values * scale, axis=0, keepdims=True)
    return back, gain_grad


def gelu_parts(u):
    root = 0.7978845608028654
    cube = 0.044715
    t = jnp.tanh(root * (u + cube * u * u * u))
    value = 0.5 * u * (1.0 + t)
    slope = 0.5 * (1.0 + t) + 0.5 * u * (1.0 - t * t) * (root * (1.0 + 3.0 * cube * u * u))
    return value, slope


def head_masks(heads):
    lane = lax.broadcasted_iota(jnp.int32, (1, heads * HEAD), 1)
    return [
        ((lane >= h * HEAD) & (lane < (h + 1) * HEAD)).astype(F32).astype(BF16)
        for h in range(heads)
    ]


def spread_heads(values, masks):
    return jnp.concatenate([values * m for m in masks], axis=0)


def join_heads(values, masks):
    rows = values.shape[0] // len(masks)
    total = None
    for h, m in enumerate(masks):
        term = values[h * rows : (h + 1) * rows] * m.astype(F32)
        total = term if total is None else total + term
    return total


def main_kernel(
    dims,
    h_ref,
    enc_ref,
    up_ref,
    w_ref,
    gain_ref,
    bias_ref,
    cmask_ref,
    bmap_ref,
    out_ref,
    ingrad_ref,
    encgrad_ref,
    grad_ref,
    gaingrad_ref,
    table_ref,
    x_in,
    g_in,
    r_one,
    r_two,
    n_one,
    n_two,
    n_three,
    qkv_s,
    so_s,
    p_s,
    cq_s,
    ckv_s,
    co_s,
    pc_s,
    gu_s,
    hid_s,
    send_one,
    recv_one,
    send_two,
    recv_two,
    enc_send,
    enc_own,
    enc_recv,
    sem_send,
    sem_recv,
    sem_enc_send,
    sem_enc_recv,
):
    layers, rows, inner, ff, heads = dims
    half = rows // 2
    t = lax.axis_index("tensor")
    near = t + 1 - 2 * (t % 2)
    far = t + 2 - 4 * ((t // 2) % 2)
    both = far + 1 - 2 * (far % 2)
    peers = (near, far, both)
    masks = head_masks(heads)
    c_q = 3 * ff
    c_so = c_q + 3 * inner
    c_cq = c_q + 4 * inner
    c_ck = c_q + 5 * inner
    c_cv = c_q + 6 * inner
    c_co = c_q + 7 * inner
    c_end = c_q + 8 * inner

    barrier = pltpu.get_barrier_semaphore()
    for peer in peers:
        pl.semaphore_signal(barrier, inc=1, device_id={"tensor": peer}, device_id_type=MESH)
    pl.semaphore_wait(barrier, 3)

    def copy_to(src, dst, sem_a, sem_b, peer):
        return pltpu.make_async_remote_copy(
            src_ref=src,
            dst_ref=dst,
            send_sem=sem_a,
            recv_sem=sem_b,
            device_id={"tensor": peer},
            device_id_type=MESH,
        )

    def all_sum(slot, make_half, cover):
        firsts = []
        for part in range(2):
            value = make_half(part).astype(BF16)
            send_one[slot, part] = value
            copy = copy_to(
                send_one.at[slot, part],
                recv_one.at[slot, part],
                sem_send.at[slot, part],
                sem_recv.at[slot, part],
                near if part == 0 else far,
            )
            copy.start()
            firsts.append(copy)
        if cover is not None:
            cover()
        seconds = []
        for part in range(2):
            firsts[part].wait()
            value = send_one[slot, part].astype(F32) + recv_one[slot, part].astype(F32)
            send_two[slot, part] = value.astype(BF16)
            copy = copy_to(
                send_two.at[slot, part],
                recv_two.at[slot, part],
                sem_send.at[slot, part + 2],
                sem_recv.at[slot, part + 2],
                far if part == 0 else near,
            )
            copy.start()
            seconds.append(copy)
        pieces = []
        for part in range(2):
            seconds[part].wait()
            pieces.append(send_two[slot, part].astype(F32) + recv_two[slot, part].astype(F32))
        return jnp.concatenate(pieces, axis=0)

    x_in[0] = h_ref[...]

    def forward(l, carry):
        x0 = x_in[l].astype(F32)
        n1 = (x0 * norm_scale(x0) * gain_ref[l, 0:1]).astype(BF16)
        n_one[l] = n1
        qkv = dot_nn(n1, w_ref[l, :, c_q:c_so]).astype(BF16)
        qkv_s[l] = qkv
        q = qkv[:, :inner]
        k = qkv[:, inner : 2 * inner]
        v = qkv[:, 2 * inner :]
        e = jnp.exp(dot_nt(spread_heads(q, masks), k) + bias_ref[l])
        p = e * (1.0 / jnp.sum(e, axis=-1, keepdims=True))
        p_s[l] = p
        so_s[l] = join_heads(dot_nn(p.astype(BF16), v), masks).astype(BF16)

        def make_one(part):
            return dot_nt(
                so_s[l, part * half : (part + 1) * half], w_ref[l, :, c_so:c_cq]
            )

        def cover_one():
            ckv_s[l] = dot_nn(enc_ref[...], w_ref[l, :, c_ck:c_co]).astype(BF16)

        x1 = x0 + all_sum(3 * l, make_one, cover_one)
        r_one[l] = x1
        n2 = (x1 * norm_scale(x1) * gain_ref[l, 1:2]).astype(BF16)
        n_two[l] = n2
        cq = dot_nn(n2, w_ref[l, :, c_cq:c_ck]).astype(BF16)
        cq_s[l] = cq
        ckv = ckv_s[l]
        ck = ckv[:, :inner]
        cv = ckv[:, inner:]
        cmask = cmask_ref[...]
        e = jnp.exp(
            dot_nt(spread_heads(cq, masks), ck) + jnp.concatenate([cmask] * heads, axis=0)
        )
        p = e * (1.0 / jnp.sum(e, axis=-1, keepdims=True))
        pc_s[l] = p
        co_s[l] = join_heads(dot_nn(p.astype(BF16), cv), masks).astype(BF16)

        def make_two(part):
            return dot_nt(
                co_s[l, part * half : (part + 1) * half], w_ref[l, :, c_co:c_end]
            )

        x2 = x1 + all_sum(3 * l + 1, make_two, None)
        r_two[l] = x2
        n3 = (x2 * norm_scale(x2) * gain_ref[l, 2:3]).astype(BF16)
        n_three[l] = n3
        gu = dot_nn(n3, w_ref[l, :, 0 : 2 * ff])
        gu_s[l] = gu
        value, _ = gelu_parts(gu[:, :ff])
        hid_s[l] = (value * gu[:, ff:]).astype(BF16)

        def make_three(part):
            return dot_nt(
                hid_s[l, part * half : (part + 1) * half], w_ref[l, :, 2 * ff : 3 * ff]
            )

        result = (x2 + all_sum(3 * l + 2, make_three, None)).astype(BF16)
        out_ref[l] = result
        x_in[l + 1] = result
        return carry

    lax.fori_loop(0, layers, forward, 0)
    g_in[...] = up_ref[...]

    def attend_back(grad, query, keys, values, attended, p):
        gs = spread_heads(grad, masks)
        qs = spread_heads(query, masks)
        delta = jnp.sum(
            gs.astype(F32) * jnp.concatenate([attended.astype(F32)] * heads, axis=0),
            axis=-1,
            keepdims=True,
        )
        ds = p * (dot_nt(gs, values) - delta)
        dsb = ds.astype(BF16)
        grad_query = join_heads(dot_nn(dsb, keys), masks).astype(BF16)
        return grad_query, ds, dsb, gs, qs

    def backward(step, carry):
        l = layers - 1 - step
        base = 3 * layers + 3 * step
        slot = (l + lax.axis_index("pipe")) % layers
        g3 = g_in[...]
        g = g3.astype(F32)
        gu = gu_s[l]
        value, slope = gelu_parts(gu[:, :ff])
        dh = dot_nn(g3, w_ref[l, :, 2 * ff : 3 * ff])
        dgu = jnp.concatenate(
            [(dh * gu[:, ff:] * slope).astype(BF16), (dh * value).astype(BF16)], axis=1
        )

        def make_three(part):
            return dot_nt(dgu[part * half : (part + 1) * half], w_ref[l, :, 0 : 2 * ff])

        def cover_three():
            grad_ref[slot, :, 0 : 2 * ff] = dot_tn(n_three[l], dgu).astype(BF16)
            grad_ref[slot, :, 2 * ff : 3 * ff] = dot_tn(g3, hid_s[l]).astype(BF16)

        dn = all_sum(base, make_three, cover_three)
        back, gain_three = norm_back(r_two[l], gain_ref[l, 2:3], dn)
        gaingrad_ref[l, 2:3] = gain_three
        g2 = g + back
        g2b = g2.astype(BF16)
        dc = dot_nn(g2b, w_ref[l, :, c_co:c_end]).astype(BF16)
        ckv = ckv_s[l]
        co = co_s[l]
        pc = pc_s[l]
        dcq, _, dsb, gs, qs = attend_back(dc, cq_s[l], ckv[:, :inner], ckv[:, inner:], co, pc)

        def make_two(part):
            return dot_nt(dcq[part * half : (part + 1) * half], w_ref[l, :, c_cq:c_ck])

        def cover_two():
            dck = dot_tn(dsb, qs).astype(BF16)
            dcv = dot_tn(pc.astype(BF16), gs).astype(BF16)
            dckv = jnp.concatenate([dck, dcv], axis=1)
            tsize = D // inner
            for k in range(tsize):
                owner = t if k == 0 else peers[k - 1]
                start = pl.multiple_of(owner * inner, HEAD)
                chunk = dot_nt(dckv, w_ref[l, pl.ds(start, inner), c_ck:c_co])
                if k == 0:
                    enc_own[l] = chunk
                else:
                    enc_send[l, k - 1] = chunk.astype(BF16)
                    copy_to(
                        enc_send.at[l, k - 1],
                        enc_recv.at[l, k - 1],
                        sem_enc_send.at[l, k - 1],
                        sem_enc_recv.at[l, k - 1],
                        peers[k - 1],
                    ).start()
            enc = enc_ref[...]
            block = jnp.concatenate([dot_tn(n_two[l], dcq), dot_tn(enc, dckv)], axis=1)
            grad_ref[slot, :, c_cq:c_co] = block.astype(BF16)
            grad_ref[slot, :, c_co:c_end] = dot_tn(g2b, co).astype(BF16)

        dn = all_sum(base + 1, make_two, cover_two)
        back, gain_two = norm_back(r_one[l], gain_ref[l, 1:2], dn)
        gaingrad_ref[l, 1:2] = gain_two
        g1 = g2 + back
        g1b = g1.astype(BF16)
        dself = dot_nn(g1b, w_ref[l, :, c_so:c_cq]).astype(BF16)
        qkv = qkv_s[l]
        so = so_s[l]
        ps = p_s[l]
        dq, ds, dsb, gs, qs = attend_back(
            dself, qkv[:, :inner], qkv[:, inner : 2 * inner], qkv[:, 2 * inner :], so, ps
        )
        dk = dot_tn(dsb, qs).astype(BF16)
        dv = dot_tn(ps.astype(BF16), gs).astype(BF16)
        dqkv = jnp.concatenate([dq, dk, dv], axis=1)

        def make_one(part):
            return dot_nt(dqkv[part * half : (part + 1) * half], w_ref[l, :, c_q:c_so])

        def cover_one():
            grad_ref[slot, :, c_q:c_cq] = jnp.concatenate(
                [dot_tn(n_one[l], dqkv), dot_tn(g1b, so)], axis=1
            ).astype(BF16)
            bmap = bmap_ref[...]
            for h in range(heads):
                ds_h = ds[h * rows : (h + 1) * rows]
                for b in range(BUCKETS):
                    table_ref[l, h, b : b + 1] = jnp.sum(
                        jnp.where(bmap == b, ds_h, 0.0), axis=0, keepdims=True
                    )

        dn = all_sum(base + 2, make_one, cover_one)
        back, gain_one = norm_back(x_in[l].astype(F32), gain_ref[l, 0:1], dn)
        gaingrad_ref[l, 0:1] = gain_one
        gin = g1 + back
        ingrad_ref[l] = gin
        g_in[...] = gin.astype(BF16)
        return carry

    lax.fori_loop(0, layers, backward, 0)
    for l in range(layers):
        total = enc_own[l]
        for k in range(3):
            copy_to(
                enc_send.at[l, k],
                enc_recv.at[l, k],
                sem_enc_send.at[l, k],
                sem_enc_recv.at[l, k],
                peers[k],
            ).wait()
            total = total + enc_recv[l, k].astype(F32)
        encgrad_ref[l] = total


def run_main(h, enc, up, w, gains, bias, cmask, bmap, inner, ff):
    layers, width = w.shape[0], w.shape[2]
    rows, enc_rows = h.shape[0], enc.shape[0]
    heads = inner // HEAD
    half = rows // 2
    slots = 6 * layers
    vm = pltpu.VMEM
    dims = (layers, rows, inner, ff, heads)
    return pl.pallas_call(
        functools.partial(main_kernel, dims),
        out_shape=(
            jax.ShapeDtypeStruct((layers, rows, D), BF16),
            jax.ShapeDtypeStruct((layers, rows, D), F32),
            jax.ShapeDtypeStruct((layers, enc_rows, inner), F32),
            jax.ShapeDtypeStruct((layers, D, width), BF16),
            jax.ShapeDtypeStruct((layers, 3, D), F32),
            jax.ShapeDtypeStruct((layers, heads, BUCKETS, rows), F32),
        ),
        in_specs=[pl.BlockSpec(memory_space=pltpu.VMEM)] * 8,
        out_specs=(pl.BlockSpec(memory_space=pltpu.VMEM),) * 6,
        scratch_shapes=[
            vm((layers + 1, rows, D), BF16),
            vm((rows, D), BF16),
            vm((layers, rows, D), F32),
            vm((layers, rows, D), F32),
            vm((layers, rows, D), BF16),
            vm((layers, rows, D), BF16),
            vm((layers, rows, D), BF16),
            vm((layers, rows, 3 * inner), BF16),
            vm((layers, rows, inner), BF16),
            vm((layers, heads * rows, rows), F32),
            vm((layers, rows, inner), BF16),
            vm((layers, enc_rows, 2 * inner), BF16),
            vm((layers, rows, inner), BF16),
            vm((layers, heads * rows, enc_rows), F32),
            vm((layers, rows, 2 * ff), F32),
            vm((layers, rows, ff), BF16),
            vm((slots, 2, half, D), BF16),
            vm((slots, 2, half, D), BF16),
            vm((slots, 2, half, D), BF16),
            vm((slots, 2, half, D), BF16),
            vm((layers, 3, enc_rows, inner), BF16),
            vm((layers, enc_rows, inner), F32),
            vm((layers, 3, enc_rows, inner), BF16),
            pltpu.SemaphoreType.DMA((slots, 4)),
            pltpu.SemaphoreType.DMA((slots, 4)),
            pltpu.SemaphoreType.DMA((layers, 3)),
            pltpu.SemaphoreType.DMA((layers, 3)),
        ],
        compiler_params=pltpu.CompilerParams(
            collective_id=0, has_side_effects=True, vmem_limit_bytes=60 * 1024 * 1024
        ),
    )(h, enc, up, w, gains, bias, cmask, bmap)


def body(
    layer_input,
    enc_states,
    out_grad,
    dec_seg,
    enc_seg,
    buckets,
    sa_q,
    sa_k,
    sa_v,
    sa_o,
    ca_q,
    ca_k,
    ca_v,
    ca_o,
    ff_gate,
    ff_up,
    ff_down,
    norm_gains,
    rel_table,
):
    layers = lax.axis_size("pipe")
    dp = lax.axis_size("dp")
    mine = lax.axis_index("pipe")
    rows = layer_input.shape[1]
    inner, ff = sa_q.shape[2], ff_gate.shape[2]
    heads = inner // HEAD
    chunk, table_rows = sa_q.shape[1], rel_table.shape[1]

    def swap(value):
        return lax.ppermute(value, "pipe", [(0, 1), (1, 0)])

    tail = jnp.zeros((chunk, TAIL), BF16)
    tail = lax.dynamic_update_slice(tail, norm_gains[0].T, (0, 0))
    tail = lax.dynamic_update_slice(tail, rel_table[0], (0, 3))
    packed = jnp.concatenate(
        [
            ff_gate[0],
            ff_up[0],
            ff_down[0].T,
            sa_q[0],
            sa_k[0],
            sa_v[0],
            sa_o[0].T,
            ca_q[0],
            ca_k[0],
            ca_v[0],
            ca_o[0].T,
            tail,
        ],
        axis=1,
    )
    width = packed.shape[1]
    w = lax.all_gather(packed, ("pipe", "dp"), axis=0, tiled=True).reshape(layers, D, width)
    tails = w[:, :, width - TAIL :].astype(F32)
    gains = tails[:, :, 0:3].transpose(0, 2, 1)
    table = tails.reshape(layers, dp, chunk, TAIL)[:, :, :table_rows, 3 : 3 + heads]
    table = table.reshape(layers, BUCKETS, heads)

    dec_ids = lax.dynamic_index_in_dim(dec_seg, mine, 0, keepdims=False)
    enc_ids = lax.dynamic_index_in_dim(enc_seg, mine, 0, keepdims=False)
    row_ids = jnp.arange(rows, dtype=jnp.int32)
    allowed_self = (dec_ids[:, None] == dec_ids[None, :]) & (row_ids[None, :] <= row_ids[:, None])
    cmask = jnp.where(dec_ids[:, None] == enc_ids[None, :], 0.0, -1e30).astype(F32)
    distance = jnp.clip(row_ids[:, None] - row_ids[None, :], 0, MAXD - 1)
    bucket_ids = jnp.arange(BUCKETS, dtype=jnp.int32)
    starts = jnp.sum((buckets[None, :] < bucket_ids[1:, None]).astype(jnp.int32), axis=1)
    bmap = jnp.sum((distance[None] >= starts[:, None, None]).astype(jnp.int32), axis=0)
    bias = jnp.sum(
        jnp.where(
            bmap[None, None, None] == bucket_ids[:, None, None, None, None],
            table.transpose(1, 0, 2)[:, :, :, None, None],
            0.0,
        ),
        axis=0,
    )
    bias = jnp.where(allowed_self[None, None], bias, -1e30).reshape(layers, heads * rows, rows)

    h = lax.dynamic_index_in_dim(layer_input, mine, 0, keepdims=False)
    enc = lax.dynamic_index_in_dim(enc_states, mine, 0, keepdims=False)
    up = lax.dynamic_index_in_dim(out_grad, mine, 0, keepdims=False)
    outs, ingrads, encgrads, grads, gain_grads, table_grads = run_main(
        h, enc, up, w, gains, bias, cmask, bmap, inner, ff
    )

    def by_micro(values, sent_type):
        own = lax.dynamic_index_in_dim(values, mine, 0, keepdims=False)
        away = lax.dynamic_index_in_dim(values, 1 - mine, 0, keepdims=False)
        got = swap(away.astype(sent_type)).astype(values.dtype)
        first = jnp.where(mine == 0, own, got)
        second = jnp.where(mine == 0, got, own)
        return jnp.stack([first, second])[None]

    table_grads = jnp.sum(table_grads, axis=-1).transpose(0, 2, 1)
    table_grads = table_grads.reshape(layers, dp, table_rows, heads)
    table_grads = jnp.pad(table_grads, ((0, 0), (0, 0), (0, chunk - table_rows), (0, 0)))
    tail_grads = jnp.concatenate(
        [gain_grads.transpose(0, 2, 1), table_grads.reshape(layers, D, heads)], axis=2
    )
    tail_grads = jnp.pad(tail_grads, ((0, 0), (0, 0), (0, TAIL - 3 - heads))).astype(BF16)
    own_tail = lax.dynamic_index_in_dim(tail_grads, mine, 0, keepdims=False)
    away_tail = lax.dynamic_index_in_dim(tail_grads, 1 - mine, 0, keepdims=False)
    away = lax.dynamic_update_slice(grads[1], away_tail, (0, width - TAIL))
    own = lax.dynamic_update_slice(grads[0], own_tail, (0, width - TAIL))
    merged = (own.astype(F32) + swap(away).astype(F32)).astype(BF16)
    summed = lax.psum_scatter(merged, "dp", scatter_dimension=0, tiled=True).astype(F32)
    base = 3 * ff

    def cut(index):
        return summed[:, base + index * inner : base + (index + 1) * inner]

    return (
        by_micro(outs, BF16),
        by_micro(ingrads, BF16),
        by_micro(encgrads, BF16),
        cut(0)[None],
        cut(1)[None],
        cut(2)[None],
        cut(3).T[None],
        cut(4)[None],
        cut(5)[None],
        cut(6)[None],
        cut(7).T[None],
        summed[None, :, 0:ff],
        summed[None, :, ff : 2 * ff],
        summed[:, 2 * ff : 3 * ff].T[None],
        summed[:, width - TAIL : width - TAIL + 3].T[None],
        summed[:table_rows, width - TAIL + 3 : width - TAIL + 3 + heads][None],
    )


def solution(mesh):
    inner_spec = P("pipe", "dp", "tensor")
    outer_spec = P("pipe", "tensor", "dp")
    placed = (
        P(None, "dp", None),
        P(None, "dp", None),
        P(None, "dp", None),
        P(None, "dp"),
        P(None, "dp"),
        P(),
        inner_spec,
        inner_spec,
        inner_spec,
        outer_spec,
        inner_spec,
        inner_spec,
        inner_spec,
        outer_spec,
        inner_spec,
        inner_spec,
        outer_spec,
        P("pipe", None, "dp"),
        inner_spec,
    )
    return jax.shard_map(
        body,
        mesh=mesh,
        in_specs=placed,
        out_specs=(
            P("pipe", None, "dp", None),
            P("pipe", None, "dp", None),
            P("pipe", None, "dp", "tensor"),
            inner_spec,
            inner_spec,
            inner_spec,
            outer_spec,
            inner_spec,
            inner_spec,
            inner_spec,
            outer_spec,
            inner_spec,
            inner_spec,
            outer_spec,
            P("pipe", None, "dp"),
            inner_spec,
        ),
        check_vma=False,
    )
```
